512 devices in a mesh: sta: 64 (over x, z_lo, core), band: 8 (over y, z_hi).
Axes of the slice: x: 4, y: 4, z: 16 (z_hi: 2, z_lo: 8; z = z_hi * 8 + z_lo), core: 2. Of those that a mesh axis runs over, the one named last changes fastest.
Arguments:
- spectra: bfloat16 [2, 8, 24576, 1024], P(None, None, 'sta', 'band')
- half_width: int32 [1024], P('band'), may hold values from 1 to 8, as said below
Outputs:
- correlations: bfloat16 [24576, 3, 32, 384], P('sta', None, 'band')
The draws below stay inside these ranges and needn't reach their ends.
Inputs may be any that keep to these rules, and one draw needn't show every extreme that they name: `half_width`: at most 8, and exactly 8 at one bin or more.
All inputs are finite; a program needn't handle non-finite values.
Results may differ from the reference program's by a relative error of at most 0.0062.
Values may be sent and summed in bfloat16 or wider, within the bound.
No kernel may reach another device: no remote copies, remote signals or barrier semaphores. Data moves between devices by JAX's collectives and lax.ppermute only.
A program may use at most 64 MiB of HBM per device.

```python
import math
import jax
import jax.numpy as jnp
from jax import lax

GRP_ST = 128
NF = 1024
SEGS = 8
ROUNDS = 3
LAGS = 4
LAG_STEP = 8
WMAX = 8
CHANNELS = 24576
N_STA = 64
N_BAND = 8


def draw_spectra(key, part):
    shape = (2, SEGS, CHANNELS, NF)
    first, second, third, fourth = jax.random.split(key, 4)
    base = jax.random.normal(first, shape, jnp.float32)
    chan_scale = jnp.exp(jax.random.uniform(second, (1, 1, CHANNELS, 1), jnp.float32, -1.15, 1.15))
    bin_scale = jnp.exp(jax.random.uniform(third, (1, 1, 1, NF), jnp.float32, -1.15, 1.15))
    rough_scale = jnp.exp(jax.random.uniform(fourth, (1, 1, CHANNELS, NF), jnp.float32, -0.7, 0.7))
    return (base * chan_scale * bin_scale * rough_scale).astype(jnp.bfloat16)


def draw_half_width(key, part):
    widths = jax.random.randint(key, (NF,), 1, WMAX + 1, jnp.int32)
    where_most = jax.random.randint(jax.random.fold_in(key, 1), (), 0, NF, jnp.int32)
    return widths.at[where_most].set(WMAX)


def setup_inputs(seed: int = 0) -> dict:
    arg_keys = jax.random.split(jax.random.key(seed), 3)
    return {
        "spectra": draw_spectra(jax.random.fold_in(arg_keys[2], 71), 0),
        "half_width": draw_half_width(jax.random.fold_in(arg_keys[2], 71), 0),
    }


def rotate_part(part, cosines, sines):
    real_part = part[0].astype(jnp.float32)[None]
    imag_part = part[1].astype(jnp.float32)[None]
    cos_block = cosines[:, None, None, :]
    sin_block = sines[:, None, None, :]
    rot_real = (real_part * cos_block - imag_part * sin_block).astype(jnp.bfloat16)
    rot_imag = (real_part * sin_block + imag_part * cos_block).astype(jnp.bfloat16)
    return jnp.stack([rot_real, rot_imag])

def reference(spectra, half_width):
    stations = GRP_ST * N_STA
    group_chans = 3 * GRP_ST
    band_bins = NF // N_BAND
    energy = lax.optimization_barrier(jnp.sum(jnp.square(spectra.astype(jnp.float32)), axis=(0, 1)))
    energy = lax.optimization_barrier(jnp.sum(energy.reshape(stations, 3, NF), axis=1))
    positions = jnp.arange(NF, dtype=jnp.int32)
    distance = jnp.abs(positions[:, None] - positions[None, :])
    window = (distance <= half_width[None, :]).astype(jnp.float32)
    window_sum = jnp.dot(energy, window, precision=lax.Precision.HIGHEST)
    counts = lax.optimization_barrier(jnp.sum(window, axis=0))
    amplitude = jnp.sqrt(window_sum / (3.0 * SEGS * counts) + 1e-06)
    whitened = (spectra.astype(jnp.float32) / jnp.repeat(amplitude, 3, axis=0)[None, None]).astype(jnp.bfloat16)
    groups = jnp.transpose(whitened.reshape(2, SEGS, N_STA, group_chans, NF), (2, 0, 1, 3, 4))
    lag_values = jnp.arange(LAGS, dtype=jnp.float32) * LAG_STEP
    phases = math.pi * lag_values[:, None] * positions.astype(jnp.float32)[None, :] / NF
    cosines = jnp.cos(phases)
    sines = jnp.sin(phases)
    norm_factor = 1.0 / math.sqrt(SEGS * band_bins)

    def one_group(group_index):
        own_part = lax.dynamic_index_in_dim(groups, group_index, 0, keepdims=False)
        left_side = own_part.astype(jnp.float32).reshape(2, SEGS, group_chans, N_BAND, band_bins)
        results = []
        for offset in range(1, ROUNDS + 1):
            partner_index = ((group_index - offset) % N_STA).astype(jnp.int32)
            partner = lax.dynamic_index_in_dim(groups, partner_index, 0, keepdims=False)
            rotated = rotate_part(partner, cosines, sines)
            right_side = rotated.astype(jnp.float32).reshape(2, LAGS, SEGS, group_chans, N_BAND, band_bins)
            summed = jnp.einsum('cspbf,clsqbf->pblq', left_side, right_side, precision=lax.Precision.HIGHEST) * norm_factor
            results.append(summed.reshape(group_chans, N_BAND * LAGS, group_chans).astype(jnp.bfloat16))
        return jnp.stack(results, axis=1)
    stacked = lax.map(one_group, jnp.arange(N_STA, dtype=jnp.int32))
    return stacked.reshape(stations * 3, ROUNDS, N_BAND * LAGS, group_chans)
```

```python
import functools
import math

import jax
import jax.numpy as jnp
from jax import lax
from jax.experimental import pallas as pl
from jax.experimental.pallas import tpu as pltpu
from jax.sharding import PartitionSpec as P


NF = 1024
ROUNDS = 3
LAGS = 4
LAG_STEP = 8
WMAX = 8
HIGH = lax.Precision.HIGHEST

VMEM_SPEC = pl.BlockSpec(memory_space=pltpu.VMEM)
SMALL = pltpu.CompilerParams(vmem_limit_bytes=24 << 20)


def even(s):
    return s % 2 == 0


def odd(s):
    return s % 2 == 1


def along_sta(value, steps, sends=lambda s: True):
    count = lax.axis_size("sta")
    return lax.ppermute(value, "sta", [(s, (s + steps) % count) for s in range(count) if sends(s)])


def along_band(value, steps):
    stas, bands = lax.axis_size("sta"), lax.axis_size("band")
    pairs = [
        (s * bands + b, s * bands + b + steps)
        for s in range(stas)
        if even(s)
        for b in range(bands)
        if 0 <= b + steps < bands
    ]
    return lax.ppermute(value, ("sta", "band"), pairs)


def repeat_matrix(stations, transpose=False):
    shape = (stations, 3 * stations) if transpose else (3 * stations, stations)
    st = lax.broadcasted_iota(jnp.int32, shape, 0 if transpose else 1)
    ch = lax.broadcasted_iota(jnp.int32, shape, 1 if transpose else 0)
    return ((ch >= 3 * st) & (ch < 3 * st + 3)).astype(jnp.float32)


def selected(even_ref, a, b):
    return jnp.where(even_ref[0] == 1, a, b)


def energy_kernel(x_ref, en_ref, low_ref, high_ref, acc_ref):
    step = pl.program_id(0)
    total = None
    parts, segs = x_ref.shape[:2]
    for seg in range(segs):
        for part in range(parts):
            value = x_ref[part, seg].astype(jnp.float32)
            total = value * value if total is None else total + value * value

    @pl.when(step == 0)
    def _():
        acc_ref[...] = total

    @pl.when(step > 0)
    def _():
        acc_ref[...] += total

    @pl.when(step == pl.num_programs(0) - 1)
    def _():
        energy = jnp.dot(
            repeat_matrix(en_ref.shape[0], True), acc_ref[...], precision=HIGH,
            preferred_element_type=jnp.float32,
        )
        turned = energy.T
        en_ref[...] = energy
        low_ref[...] = turned[:WMAX]
        high_ref[...] = turned[turned.shape[0] - WMAX :]


def energies(x, steps=4):
    parts, segs, chans, bins = x.shape
    stations = chans // 3
    rim = jax.ShapeDtypeStruct((WMAX, stations), jnp.float32)
    return pl.pallas_call(
        energy_kernel,
        grid=(steps,),
        in_specs=[pl.BlockSpec((parts, segs // steps, chans, bins), lambda s: (0, s, 0, 0))],
        out_specs=[
            pl.BlockSpec((stations, bins), lambda s: (0, 0)),
            pl.BlockSpec((WMAX, stations), lambda s: (0, 0)),
            pl.BlockSpec((WMAX, stations), lambda s: (0, 0)),
        ],
        out_shape=[jax.ShapeDtypeStruct((stations, bins), jnp.float32), rim, rim],
        scratch_shapes=[pltpu.VMEM((chans, bins), jnp.float32)],
        compiler_params=SMALL,
        name="energies",
    )(x)


def edges_kernel(own_low, own_high, other_ref, low_ref, high_ref):
    other = other_ref[...].T
    stations = own_low.shape[1]
    low_ref[:, :stations] = own_low[...]
    low_ref[:, stations:] = other[:WMAX]
    high_ref[:, :stations] = own_high[...]
    high_ref[:, stations:] = other[other.shape[0] - WMAX :]


def edges(own_low, own_high, other):
    shape = pltpu.VMEM((WMAX, 2 * other.shape[0]), jnp.float32)
    return pl.pallas_call(
        edges_kernel,
        in_specs=[VMEM_SPEC] * 3,
        out_specs=[VMEM_SPEC] * 2,
        out_shape=[shape, shape],
        compiler_params=SMALL,
        name="edges",
    )(own_low, own_high, other)


def inverse_kernel(segs, first_ref, own_ref, other_ref, below_ref, above_ref, width_ref, out_ref):
    _, bins = own_ref.shape
    first = first_ref[0]
    width = width_ref[...]
    inner = lax.broadcasted_iota(jnp.int32, (bins, bins), 0)
    target = lax.broadcasted_iota(jnp.int32, (bins, bins), 1)
    window = (jnp.abs(inner - target) <= width).astype(jnp.float32)
    rim = lax.broadcasted_iota(jnp.int32, (WMAX, bins), 0)
    rim_target = lax.broadcasted_iota(jnp.int32, (WMAX, bins), 1)
    window_below = (rim_target - (rim - WMAX) <= width).astype(jnp.float32)
    window_above = (rim + bins - rim_target <= width).astype(jnp.float32)
    energy = jnp.concatenate([own_ref[...], other_ref[...]], axis=0)
    rims = jnp.concatenate([below_ref[...], above_ref[...]], axis=0)
    rim_window = jnp.concatenate([window_below, window_above], axis=0)
    sums = jnp.dot(energy, window, precision=HIGH, preferred_element_type=jnp.float32)
    sums += jnp.dot(rims.T, rim_window, precision=HIGH, preferred_element_type=jnp.float32)
    bin_index = first + lax.broadcasted_iota(jnp.int32, (1, bins), 1)
    counts = jnp.minimum(bin_index + width, NF - 1) - jnp.maximum(bin_index - width, 0) + 1
    amplitude = jnp.sqrt(sums / (3.0 * segs * counts.astype(jnp.float32)) + 1e-06)
    out_ref[...] = 1.0 / amplitude


def inverses(first_bin, own, other, below, above, half_width, segs):
    stations, bins = own.shape
    return pl.pallas_call(
        functools.partial(inverse_kernel, segs),
        in_specs=[pl.BlockSpec(memory_space=pltpu.SMEM)] + [VMEM_SPEC] * 5,
        out_specs=VMEM_SPEC,
        out_shape=pltpu.VMEM((2 * stations, bins), jnp.float32),
        compiler_params=SMALL,
        name="inverses",
    )(first_bin.reshape(1), own, other, below, above, half_width.reshape(1, bins))


def widened(inverse, chans_at=0, chans=None):
    full = repeat_matrix(inverse.shape[0])
    if chans is not None:
        full = full[chans_at : chans_at + chans]
    return jnp.dot(full, inverse, precision=HIGH, preferred_element_type=jnp.float32)


def rotate_kernel(even_ref, x_ref, inverse_ref, shared_ref, table_ref, out_ref, mix_ref):
    parts, segs, chans, bins = x_ref.shape
    stations = chans // 3
    wide = widened(selected(even_ref, inverse_ref[:stations], shared_ref[stations:]))
    for seg in range(segs):
        real = (x_ref[0, seg].astype(jnp.float32) * wide).astype(jnp.bfloat16).astype(jnp.float32)
        imag = (x_ref[1, seg].astype(jnp.float32) * wide).astype(jnp.bfloat16).astype(jnp.float32)
        for lag in range(LAGS):
            cos = table_ref[lag : lag + 1, :]
            sin = table_ref[LAGS + lag : LAGS + lag + 1, :]
            mix_ref[seg % 2, 0, pl.ds(lag, chans, stride=LAGS), :] = real * cos + imag * sin
            mix_ref[seg % 2, 1, pl.ds(lag, chans, stride=LAGS), :] = imag * cos - real * sin
        for part in range(parts):
            at = (seg * parts + part) * bins
            out_ref[:, at : at + bins] = mix_ref[seg % 2, part].astype(jnp.bfloat16)


def rotated(even, x, inverse, shared, table):
    parts, segs, chans, bins = x.shape
    return pl.pallas_call(
        rotate_kernel,
        in_specs=[pl.BlockSpec(memory_space=pltpu.SMEM)] + [VMEM_SPEC] * 4,
        out_specs=VMEM_SPEC,
        out_shape=pltpu.VMEM((LAGS * chans, segs * parts * bins), jnp.bfloat16),
        scratch_shapes=[pltpu.VMEM((2, parts, LAGS * chans, bins), jnp.float32)],
        compiler_params=SMALL,
        name="rotated",
    )(even, x, inverse, shared, table)


def round_kernel(norm_factor, at, picks, rows, even_ref, left_ref, *refs):
    partner_refs = refs[: len(picks)]
    inverse_refs = refs[len(picks) : len(picks) + 2]
    out_ref, right_ref = refs[-2:]
    parts, segs, bins = partner_refs[0].shape[0], partner_refs[0].shape[1], partner_refs[0].shape[3]
    chans = right_ref.shape[0]
    step = pl.program_id(0)

    @pl.when(step == 0)
    def _():
        (a_ref, a_at), (b_ref, b_at) = zip(inverse_refs, at[1])
        stations = left_ref.shape[0] // (3 * LAGS)
        inverse = selected(even_ref, a_ref[a_at : a_at + stations], b_ref[b_at : b_at + stations])
        wide = widened(inverse, at[0], chans)
        for seg in range(segs):
            for part in range(parts):
                value = None
                for ref, pick in zip(partner_refs, picks):
                    piece = ref[part, seg, pick : pick + chans].astype(jnp.float32)
                    value = piece if value is None else value + piece
                to = (seg * parts + part) * bins
                right_ref[:, to : to + bins] = (value * wide).astype(jnp.bfloat16)

    begin = pl.multiple_of(step * (LAGS * rows), LAGS * rows)
    summed = lax.dot_general(
        left_ref[pl.ds(begin, LAGS * rows), :], right_ref[...], (((1,), (1,)), ((), ())),
        preferred_element_type=jnp.float32,
    )
    out_ref[...] = (summed * norm_factor).astype(jnp.bfloat16).reshape(out_ref.shape)


def one_round(even, left, partners, inverse_pair, index, norm_factor, previous=None,
              chans=None, at=0, rows=192):
    parts, segs, _, bins = partners[0][0].shape
    every = left.shape[0] // LAGS
    chans = every if chans is None else chans
    operands = [even, left, *[p for p, _ in partners], *[v for v, _ in inverse_pair]]
    in_specs = [pl.BlockSpec(memory_space=pltpu.SMEM)] + [VMEM_SPEC] * (len(operands) - 1)
    aliases = {}
    if previous is not None:
        aliases = {len(operands): 0}
        operands.append(previous)
        in_specs.append(pl.BlockSpec(memory_space=pl.ANY))
    return pl.pallas_call(
        functools.partial(
            round_kernel, norm_factor, (at, [r for _, r in inverse_pair]), [k for _, k in partners], rows
        ),
        grid=(every // rows,),
        in_specs=in_specs,
        out_specs=pl.BlockSpec((rows, 1, LAGS, chans), lambda i: (i, index, 0, at // chans)),
        out_shape=jax.ShapeDtypeStruct((every, ROUNDS, LAGS, every), jnp.bfloat16),
        scratch_shapes=[pltpu.VMEM((chans, parts * segs * bins), jnp.bfloat16)],
        input_output_aliases=aliases,
        compiler_params=SMALL,
        name="one_round",
    )(*operands)


def shards(spectra, half_width):
    segs = spectra.shape[1]
    chans = spectra.shape[2]
    bins = spectra.shape[3]
    stations = chans // 3
    even_flag = (1 - lax.rem(lax.axis_index("sta"), 2)).astype(jnp.int32).reshape(1)
    first_bin = lax.axis_index("band") * bins
    lag_values = jnp.arange(LAGS, dtype=jnp.float32) * LAG_STEP
    inner = first_bin + jnp.arange(bins, dtype=jnp.int32)
    phases = math.pi * lag_values[:, None] * inner.astype(jnp.float32)[None, :] / NF
    table = jnp.concatenate([jnp.cos(phases), jnp.sin(phases)], axis=0)
    norm_factor = 1.0 / math.sqrt(segs * bins)
    head = 2 * chans // 3

    first = along_sta(spectra, 1)
    energy, low, high = energies(spectra)
    other = along_sta(energy, -1, odd)
    low, high = edges(low, high, other)
    below = along_band(high, 1)
    above = along_band(low, -1)
    inverse = inverses(first_bin, energy, other, below, above, half_width, segs)
    before = along_sta(inverse, 2, even)
    shared = along_sta(inverse, 1, even)
    third_odd = along_sta(first, 2, odd)
    third_head = along_sta(first[:, :, :head], 2, even)
    left = rotated(even_flag, spectra, inverse, shared, table)
    third_inverse = along_sta(inverse[stations:], 4, even)
    third_tail = along_sta(first[:, :, head:], 2, even)
    second_odd = along_sta(first, 1, even)
    shared_before = along_sta(before, 1, even)
    out = one_round(
        even_flag, left, [(first, 0)], [(before, stations), (shared, 0)], 0, norm_factor
    )
    second_even = along_sta(third_odd, -1, odd)
    out = one_round(
        even_flag, left, [(second_odd, 0), (second_even, 0)],
        [(before, 0), (shared_before, stations)], 1, norm_factor, out,
    )
    pair = [(third_inverse, 0), (shared_before, 0)]
    out = one_round(
        even_flag, left, [(third_head, 0), (third_odd, 0)], pair, 2, norm_factor, out, head, 0
    )
    out = one_round(
        even_flag, left, [(third_tail, 0), (third_odd, head)], pair, 2, norm_factor, out,
        chans - head, head,
    )
    return out


def solution(mesh):
    in_specs = (P(None, None, "sta", "band"), P("band"))
    out_specs = P("sta", None, "band", None)
    return jax.shard_map(shards, mesh=mesh, in_specs=in_specs, out_specs=out_specs, check_vma=False)
```

```python
import functools
import math

import jax
import jax.numpy as jnp
from jax import lax
from jax.experimental import pallas as pl
from jax.experimental.pallas import tpu as pltpu
from jax.sharding import PartitionSpec as P


NF = 1024
ROUNDS = 3
LAGS = 4
LAG_STEP = 8
WMAX = 8
HIGH = lax.Precision.HIGHEST

VMEM_SPEC = pl.BlockSpec(memory_space=pltpu.VMEM)
SMALL = pltpu.CompilerParams(vmem_limit_bytes=14 << 20)
PACKED = pltpu.CompilerParams(vmem_limit_bytes=14 << 20)


def even(s):
    return s % 2 == 0


def odd(s):
    return s % 2 == 1


def along_sta(value, steps, sends=lambda s: True):
    count = lax.axis_size("sta")
    return lax.ppermute(value, "sta", [(s, (s + steps) % count) for s in range(count) if sends(s)])


def sends_rims_first(s, b):
    return b % 2 == (0 if (s // 2) % 8 == 5 else 1)


def along_band(value, steps, first):
    stas, bands = lax.axis_size("sta"), lax.axis_size("band")
    pairs = [
        (s * bands + b, s * bands + b + steps)
        for s in range(stas)
        if even(s)
        for b in range(bands)
        if 0 <= b + steps < bands and sends_rims_first(s, b) == first
    ]
    return lax.ppermute(value, ("sta", "band"), pairs)


def repeat_matrix(stations, transpose=False):
    shape = (stations, 3 * stations) if transpose else (3 * stations, stations)
    st = lax.broadcasted_iota(jnp.int32, shape, 0 if transpose else 1)
    ch = lax.broadcasted_iota(jnp.int32, shape, 1 if transpose else 0)
    return ((ch >= 3 * st) & (ch < 3 * st + 3)).astype(jnp.float32)


def selected(even_ref, a, b):
    return jnp.where(even_ref[0] == 1, a, b)


def energy_kernel(x_ref, en_ref, low_ref, high_ref, acc_ref):
    step = pl.program_id(0)
    total = None
    parts, segs = x_ref.shape[:2]
    for seg in range(segs):
        for part in range(parts):
            value = x_ref[part, seg].astype(jnp.float32)
            total = value * value if total is None else total + value * value

    @pl.when(step == 0)
    def _():
        acc_ref[...] = total

    @pl.when(step > 0)
    def _():
        acc_ref[...] += total

    @pl.when(step == pl.num_programs(0) - 1)
    def _():
        energy = jnp.dot(
            repeat_matrix(en_ref.shape[0], True), acc_ref[...], precision=HIGH,
            preferred_element_type=jnp.float32,
        )
        turned = energy.T
        en_ref[...] = energy
        low_ref[...] = turned[:WMAX]
        high_ref[...] = turned[turned.shape[0] - WMAX :]


def energies(x, steps=4):
    parts, segs, chans, bins = x.shape
    stations = chans // 3
    rim = jax.ShapeDtypeStruct((WMAX, stations), jnp.float32)
    return pl.pallas_call(
        energy_kernel,
        grid=(steps,),
        in_specs=[pl.BlockSpec((parts, segs // steps, chans, bins), lambda s: (0, s, 0, 0))],
        out_specs=[
            pl.BlockSpec((stations, bins), lambda s: (0, 0)),
            pl.BlockSpec((WMAX, stations), lambda s: (0, 0)),
            pl.BlockSpec((WMAX, stations), lambda s: (0, 0)),
        ],
        out_shape=[jax.ShapeDtypeStruct((stations, bins), jnp.float32), rim, rim],
        scratch_shapes=[pltpu.VMEM((chans, bins), jnp.float32)],
        compiler_params=SMALL,
        name="energies",
    )(x)


def edges_kernel(own_low, own_high, other_ref, low_ref, high_ref):
    other = other_ref[...].T
    stations = own_low.shape[1]
    low_ref[:, :stations] = own_low[...]
    low_ref[:, stations:] = other[:WMAX]
    high_ref[:, :stations] = own_high[...]
    high_ref[:, stations:] = other[other.shape[0] - WMAX :]


def edges(own_low, own_high, other):
    shape = pltpu.VMEM((WMAX, 2 * other.shape[0]), jnp.float32)
    return pl.pallas_call(
        edges_kernel,
        in_specs=[VMEM_SPEC] * 3,
        out_specs=[VMEM_SPEC] * 2,
        out_shape=[shape, shape],
        compiler_params=SMALL,
        name="edges",
    )(own_low, own_high, other)


def inverse_kernel(segs, first_ref, even_ref, table_ref, own_ref, other_ref, *refs):
    below, above = refs[0][...] + refs[2][...], refs[1][...] + refs[3][...]
    width_ref, out_ref = refs[4:]
    _, bins = own_ref.shape
    first = first_ref[0]
    width = width_ref[...]
    inner = lax.broadcasted_iota(jnp.int32, (bins, bins), 0)
    target = lax.broadcasted_iota(jnp.int32, (bins, bins), 1)
    window = (jnp.abs(inner - target) <= width).astype(jnp.float32)
    rim = lax.broadcasted_iota(jnp.int32, (WMAX, bins), 0)
    rim_target = lax.broadcasted_iota(jnp.int32, (WMAX, bins), 1)
    window_below = (rim_target - (rim - WMAX) <= width).astype(jnp.float32)
    window_above = (rim + bins - rim_target <= width).astype(jnp.float32)
    energy = jnp.concatenate([own_ref[...], other_ref[...]], axis=0)
    rims = jnp.concatenate([below, above], axis=0)
    rim_window = jnp.concatenate([window_below, window_above], axis=0)
    sums = jnp.dot(energy, window, precision=HIGH, preferred_element_type=jnp.float32)
    sums += jnp.dot(rims.T, rim_window, precision=HIGH, preferred_element_type=jnp.float32)
    bin_index = first + lax.broadcasted_iota(jnp.int32, (1, bins), 1)
    counts = jnp.minimum(bin_index + width, NF - 1) - jnp.maximum(bin_index - width, 0) + 1
    amplitude = jnp.sqrt(sums / (3.0 * segs * counts.astype(jnp.float32)) + 1e-06)
    out_ref[...] = 1.0 / amplitude


def inverses(first_bin, even, table, own, other, rims, half_width, segs):
    stations, bins = own.shape
    return pl.pallas_call(
        functools.partial(inverse_kernel, segs),
        in_specs=[pl.BlockSpec(memory_space=pltpu.SMEM)] * 2 + [VMEM_SPEC] * (4 + len(rims)),
        out_specs=VMEM_SPEC,
        out_shape=pltpu.VMEM((2 * stations, bins), jnp.float32),
        compiler_params=SMALL,
        name="inverses",
    )(first_bin.reshape(1), even, table, own, other, *rims, half_width.reshape(1, bins))


def widened(inverse):
    full = repeat_matrix(inverse.shape[0])
    return jnp.dot(full, inverse, precision=HIGH, preferred_element_type=jnp.float32)


def rotate_kernel(even_ref, x_ref, inverse_ref, shared_ref, table_ref, out_ref, mix_ref):
    parts, segs, chans, bins = x_ref.shape
    stations = chans // 3
    wide = widened(selected(even_ref, inverse_ref[:stations], shared_ref[stations:]))
    for seg in range(segs):
        real = (x_ref[0, seg].astype(jnp.float32) * wide).astype(jnp.bfloat16).astype(jnp.float32)
        imag = (x_ref[1, seg].astype(jnp.float32) * wide).astype(jnp.bfloat16).astype(jnp.float32)
        for lag in range(LAGS):
            cos = table_ref[lag : lag + 1, :]
            sin = table_ref[LAGS + lag : LAGS + lag + 1, :]
            mix_ref[seg % 2, 0, pl.ds(lag, chans, stride=LAGS), :] = real * cos + imag * sin
            mix_ref[seg % 2, 1, pl.ds(lag, chans, stride=LAGS), :] = imag * cos - real * sin
        for part in range(parts):
            at = (seg * parts + part) * bins
            out_ref[:, at : at + bins] = mix_ref[seg % 2, part].astype(jnp.bfloat16)


def rotated(even, x, inverse, shared, table):
    parts, segs, chans, bins = x.shape
    return pl.pallas_call(
        rotate_kernel,
        in_specs=[pl.BlockSpec(memory_space=pltpu.SMEM)] + [VMEM_SPEC] * 4,
        out_specs=VMEM_SPEC,
        out_shape=pltpu.VMEM((LAGS * chans, segs * parts * bins), jnp.bfloat16),
        scratch_shapes=[pltpu.VMEM((2, parts, LAGS * chans, bins), jnp.float32)],
        compiler_params=SMALL,
        name="rotated",
    )(even, x, inverse, shared, table)


def round_kernel(norm_factor, index, pieces, starts, count, even_ref, left_ref, *refs):
    partner_refs, (even_inverse, odd_inverse) = refs[:count], refs[count : count + 2]
    out_ref, right_ref, stage_ref, sems = refs[-4:]
    parts, segs, chans, bins = partner_refs[0].shape
    stations = chans // 3
    inverse = selected(
        even_ref,
        even_inverse[starts[0] : starts[0] + stations],
        odd_inverse[starts[1] : starts[1] + stations],
    )
    wide = widened(inverse)
    for seg in range(segs):
        for part in range(parts):
            value = partner_refs[0][part, seg].astype(jnp.float32)
            for ref in partner_refs[1:]:
                value = value + ref[part, seg].astype(jnp.float32)
            to = (seg * parts + part) * bins
            right_ref[:, to : to + bins] = (value * wide).astype(jnp.bfloat16)
    rows = chans // pieces
    copies = []
    for piece in range(pieces):
        summed = lax.dot_general(
            left_ref[piece * LAGS * rows : (piece + 1) * LAGS * rows, :], right_ref[...],
            (((1,), (1,)), ((), ())), preferred_element_type=jnp.float32,
        )
        here = pl.ds(piece * rows, rows)
        stage_ref[here] = (summed * norm_factor).astype(jnp.bfloat16).reshape(rows, LAGS, chans)
        copy = pltpu.make_async_copy(stage_ref.at[here], out_ref.at[here, index], sems.at[piece])
        copy.start()
        copies.append(copy)
    for copy in copies:
        copy.wait()


def one_round(even, left, partners, inverse_pair, index, norm_factor, previous=None, pieces=4):
    parts, segs, chans, bins = partners[0].shape
    operands = [even, left, *partners, *[v for v, _ in inverse_pair]]
    in_specs = [pl.BlockSpec(memory_space=pltpu.SMEM)] + [VMEM_SPEC] * (len(operands) - 1)
    aliases = {}
    if previous is not None:
        aliases = {len(operands): 0}
        operands.append(previous)
        in_specs.append(pl.BlockSpec(memory_space=pl.ANY))
    starts = [r for _, r in inverse_pair]
    return pl.pallas_call(
        functools.partial(round_kernel, norm_factor, index, pieces, starts, len(partners)),
        in_specs=in_specs,
        out_specs=pl.BlockSpec(memory_space=pl.ANY),
        out_shape=jax.ShapeDtypeStruct((chans, ROUNDS, LAGS, chans), jnp.bfloat16),
        scratch_shapes=[
            pltpu.VMEM((chans, parts * segs * bins), jnp.bfloat16),
            pltpu.VMEM((chans, LAGS, chans), jnp.bfloat16),
            pltpu.SemaphoreType.DMA((pieces,)),
        ],
        input_output_aliases=aliases,
        compiler_params=PACKED,
        name="one_round",
    )(*operands)


def shards(spectra, half_width):
    segs = spectra.shape[1]
    chans = spectra.shape[2]
    bins = spectra.shape[3]
    stations = chans // 3
    even_flag = (1 - lax.rem(lax.axis_index("sta"), 2)).astype(jnp.int32).reshape(1)
    first_bin = lax.axis_index("band") * bins
    lag_values = jnp.arange(LAGS, dtype=jnp.float32) * LAG_STEP
    inner = first_bin + jnp.arange(bins, dtype=jnp.int32)
    phases = math.pi * lag_values[:, None] * inner.astype(jnp.float32)[None, :] / NF
    table = jnp.concatenate([jnp.cos(phases), jnp.sin(phases)], axis=0)
    norm_factor = 1.0 / math.sqrt(segs * bins)

    first = along_sta(spectra, 1)
    energy, low, high = energies(spectra)
    other = along_sta(energy, -1, odd)
    low, high = edges(low, high, other)
    rims = [along_band(high, 1, True)]
    rims.append(along_band(low, -1, True))
    rims.append(along_band(high, 1, False))
    rims.append(along_band(low, -1, False))
    inverse = inverses(first_bin, even_flag, table, energy, other, rims, half_width, segs)
    before = along_sta(inverse, 2, even)
    third_odd = along_sta(first, 2, odd)
    third_even = along_sta(first, 2, even)
    shared = along_sta(inverse, 1, even)
    left = rotated(even_flag, spectra, inverse, shared, table)
    second_odd = along_sta(first, 1, even)
    shared_before = along_sta(before, 1, even)
    out = one_round(even_flag, left, [first], [(before, stations), (shared, 0)], 0, norm_factor)
    second_even = along_sta(third_odd, -1, odd)
    third_inverse = along_sta(shared_before[stations:], 1, odd)
    out = one_round(
        even_flag, left, [second_odd, second_even],
        [(before, 0), (shared_before, stations)], 1, norm_factor, out,
    )
    out = one_round(
        even_flag, left, [third_even, third_odd],
        [(third_inverse, 0), (shared_before, 0)], 2, norm_factor, out,
    )
    return out


def solution(mesh):
    in_specs = (P(None, None, "sta", "band"), P("band"))
    out_specs = P("sta", None, "band", None)
    return jax.shard_map(shards, mesh=mesh, in_specs=in_specs, out_specs=out_specs, check_vma=False)
```
